32 devices in a mesh: groups: 2 (over x), depth: 16 (over z, y, core).
Axes of the slice: x: 2, y: 2, z: 4, core: 2. Of those that a mesh axis runs over, the one named last changes fastest.
Arguments:
- fronts: bfloat16 [4, 64, 8, 2048], P(None, ('groups', 'depth')), parts along dimension 1, may hold values from -6 to 6
- extrap: bfloat16 [32, 16, 5, 2, 128, 128], P('depth'), may hold values from -0.15625 to 0.15625
- offsets: int32 [2, 5], replicated, may hold values from -2 to 2
- assign: int32 [2, 8], replicated, may hold values from 0 to 7, each once within a row
Outputs:
- images: float32 [8, 32, 2048], P(None, ('groups', 'depth')), parts along dimension 1
- last_fronts: bfloat16 [4, 64, 8, 2048], P(None, ('groups', 'depth')), parts along dimension 1
The draws below stay inside these ranges and needn't reach their ends.
There are 2 independent parts, one for each index of `groups`. The reference program is written for one: setup_inputs(seed, part) draws one part's arguments, and reference() takes and returns one part's arrays. A program takes and returns all parts, laid end to end along the dimension named above; an argument that names none is the same for every part. Nothing has to cross between parts.
Inputs may be any that keep to these rules, and one draw needn't show every extreme that they name: `assign`: each row names every shot number once.
All inputs are finite; a program needn't handle non-finite values.
Results may differ from the reference program's by a relative error of at most 0.015.
Values may be sent and summed in bfloat16 or wider, within the bound.
A program may use at most 64 MiB of HBM per device.

```python
import math
import jax
import jax.numpy as jnp
from jax import lax

BLOCK = 128
NBLK = 16
BAND = 5
HANDOVERS = 8
SHOTS = 8
X = 2048
NFREQ = 16
SECTIONS = 2


def plant(result, own_key, smallest, top_value):
    longest = result.shape.index(max(result.shape))
    spots = []
    for shift in (0, 1):
        where = [jax.random.randint(jax.random.fold_in(own_key, axis), (), 0, length) for axis, length in enumerate(result.shape)]
        where[longest] = (where[longest] + shift) % result.shape[longest]
        spots.append(tuple(where))
    return result.at[spots[0]].set(smallest).at[spots[1]].set(top_value)


def block_scale(own_key, extent, split, least, high):
    gain, own = 1.0, jax.random.fold_in(own_key, 6)
    for position, parts in split:
        draws = jnp.exp(jax.random.uniform(jax.random.fold_in(own, position), (parts,), jnp.float32, least / len(split), high / len(split)))
        gain = gain * jnp.repeat(draws, extent[position] // parts).reshape([-1 if axis == position else 1 for axis in range(len(extent))])
    return gain


def noise(own_key, shape, spread, limit, cuts=(), kind=jnp.bfloat16):
    drawn = spread * jax.random.normal(own_key, shape, jnp.float32)
    if cuts:
        drawn = drawn * block_scale(own_key, shape, cuts, -0.22, 0.18)
    return jnp.clip(drawn, -limit, limit).astype(kind)


def setup_inputs(seed: int = 0, part: int = 0) -> dict:
    keys = jax.random.split(jax.random.key(seed), 5)
    part_keys = jax.random.split(jax.random.fold_in(keys[4], part), 5)
    return {
        "fronts": noise(part_keys[0], (4, SECTIONS * NFREQ, SHOTS, X), 1.0, 6.0, ((1, 16),)),
        "extrap": noise(keys[1], (SECTIONS * NFREQ, NBLK, BAND, 2, BLOCK, BLOCK), (2 * BAND * BLOCK) ** -0.5, 0.15625, ((0, 16),)),
        "offsets": plant(jax.random.randint(keys[2], (SECTIONS, BAND), -(BAND // 2), BAND // 2 + 1), jax.random.fold_in(keys[2], 1), -(BAND // 2), (BAND // 2 + 1) - 1).astype(jnp.int32),
        "assign": jax.vmap(lambda own: jax.random.permutation(own, SHOTS))(jax.random.split(keys[3], SECTIONS)).reshape((SECTIONS, SHOTS)).astype(jnp.int32),
    }


def advance(wave_state, band_offsets, operator):
    reach = BAND // 2
    blocks = wave_state.reshape(4, NFREQ, SHOTS, NBLK, BLOCK)
    padded = jnp.pad(blocks, ((0, 0), (0, 0), (0, 0), (reach, reach), (0, 0)))
    shifted = jnp.stack([lax.dynamic_slice_in_dim(padded, band_offsets[band_pos] + reach, NBLK, 3) for band_pos in range(BAND)], axis=3)
    products = jnp.einsum('cfskbj,fbkpjl->pcfsbl', shifted.astype(jnp.float32), operator.astype(jnp.float32), precision=lax.Precision.HIGHEST)
    real_prod = products[0]
    imag_prod = products[1]
    src_real = real_prod[0] - imag_prod[1]
    src_imag = imag_prod[0] + real_prod[1]
    rec_real = real_prod[2] + imag_prod[3]
    rec_imag = real_prod[3] - imag_prod[2]
    joined = jnp.stack([src_real, src_imag, rec_real, rec_imag])
    return joined.reshape(4, NFREQ, SHOTS, X).astype(jnp.bfloat16)

def reference(fronts, extrap, offsets, assign):
    operators = extrap.reshape(SECTIONS, NFREQ, NBLK, BAND, 2, BLOCK, BLOCK)
    wave_state = jnp.moveaxis(fronts.reshape(4, SECTIONS, NFREQ, SHOTS, X), 1, 0)
    image_scale = 1.0 / math.sqrt(2.0 * NFREQ)
    section_rows = jnp.arange(SECTIONS, dtype=jnp.int32)[:, None]
    images = []
    for handover in range(HANDOVERS):
        wave_state = lax.map(lambda section_item: advance(section_item[0], section_item[1], section_item[2]), (wave_state, offsets, operators))
        fields = wave_state.astype(jnp.float32)
        partial_value = image_scale * lax.optimization_barrier(jnp.sum(fields[:, 0] * fields[:, 2] + fields[:, 1] * fields[:, 3], axis=1))
        placed = jnp.zeros_like(partial_value).at[section_rows, assign].set(partial_value)
        images.append(placed.reshape(SECTIONS * SHOTS, X))
        if handover + 1 < HANDOVERS:
            wave_state = jnp.concatenate([wave_state[-1:], wave_state[:-1]], axis=0)
    last_fronts = jnp.moveaxis(wave_state, 0, 1).reshape(4, SECTIONS * NFREQ, SHOTS, X)
    return (jnp.stack(images), last_fronts)
```

```python
import functools
import math

import jax
import jax.numpy as jnp
from jax import lax
from jax.experimental import pallas as pl
from jax.experimental.pallas import tpu as pltpu
from jax.sharding import PartitionSpec as P

HANDOVERS = 8
GROUP_ENDS = (2, 6, 12)
PART_ENDS = (2, 8, 14)
TAIL_ENDS = (8,)
LAG = 2
DEEP = 3
VMEM_BYTES = 48 << 20
STORE_BYTES = 1 << 20
MESH = pl.DeviceIdType.MESH


def cuts(total, ends):
    edges = [0] + [e for e in ends if 0 < e < total] + [total]
    return list(zip(edges[:-1], edges[1:]))


def kernel(
    sections,
    owners,
    offsets_hbm,
    assign_hbm,
    fronts_hbm,
    extrap_hbm,
    images_ref,
    last_ref,
    offsets_ref,
    assign_ref,
    fronts_ref,
    oper,
    padded,
    outbox,
    inbox,
    half_image,
    slot_image,
    share_out,
    share_in,
    table_sem,
    front_sem,
    load_sem,
    wave_send,
    wave_recv,
    share_send,
    share_recv,
):
    nfield, freqs, slots, _ = fronts_ref.shape
    nblk, band, block = oper.shape[1], oper.shape[2], oper.shape[-1]
    reach = band // 2
    scale = 1.0 / math.sqrt(2.0 * freqs * owners)
    final = HANDOVERS - 1
    me = lax.axis_index("depth")
    depth = sections * owners
    section = me // owners
    owner = me % owners
    ahead = (me + owners) % depth
    behind = (me + depth - owners) % depth

    groups = cuts(nblk, GROUP_ENDS)
    parts = cuts(nblk, PART_ENDS)
    tails = cuts(nblk, TAIL_ENDS)
    wave_slots = wave_send.shape[0]
    share_slots = 2 * LAG

    def any_mate(step):
        return section * owners + (owner + step) % owners

    barrier = pltpu.get_barrier_semaphore()
    greeted = [ahead] + ([behind] if sections > 2 else [])
    greeted = greeted + [any_mate(d) for d in range(1, owners)]
    for device in greeted:
        pl.semaphore_signal(barrier, inc=1, device_id={"depth": device}, device_id_type=MESH)

    offsets_load = pltpu.make_async_copy(offsets_hbm, offsets_ref, table_sem.at[0])
    assign_load = pltpu.make_async_copy(assign_hbm, assign_ref, table_sem.at[1])

    def front_load(freq):
        return pltpu.make_async_copy(
            fronts_hbm.at[:, freq], fronts_ref.at[:, freq], front_sem.at[freq]
        )

    def load(freq, part):
        lo, hi = groups[part]
        rows = pl.ds(lo, hi - lo)
        return pltpu.make_async_copy(
            extrap_hbm.at[freq, rows], oper.at[freq, rows], load_sem.at[freq, part]
        )

    queue = [(freq, part) for freq in range(freqs) for part in range(len(groups))]
    offsets_load.start()
    front_load(0).start()
    load(*queue[0]).start()
    assign_load.start()

    blank = jnp.zeros((reach,) + padded.shape[2:], padded.dtype)
    for freq in range(freqs):
        padded[freq, 0:reach] = blank
        padded[freq, reach + nblk : 2 * reach + nblk] = blank

    offsets_load.wait()
    assign_load.wait()
    for ahead_of in queue[1:DEEP]:
        load(*ahead_of).start()
    for freq in range(1, freqs):
        front_load(freq).start()
    offs = [offsets_ref[section, k] + reach for k in range(band)]
    slot_of = []
    for shot in range(slots):
        found = jnp.int32(0)
        for slot in range(slots):
            found = jnp.where(assign_ref[section, slot] == shot, slot, found)
        slot_of.append(found)

    def slot_for(target):
        chosen = slot_of[0]
        for shot in range(1, slots):
            chosen = jnp.where(target == shot, slot_of[shot], chosen)
        return chosen

    def unpack_front(freq):
        front_load(freq).wait()
        for b in range(nblk):
            cols = slice(b * block, (b + 1) * block)
            rows = [fronts_ref[c, freq, :, cols].astype(jnp.float32) for c in range(nfield)]
            padded[freq, reach + b] = jnp.concatenate(rows, axis=0).astype(padded.dtype)

    def remote(src, dst, send, recv, device):
        return pltpu.make_async_remote_copy(
            src_ref=src,
            dst_ref=dst,
            send_sem=send,
            recv_sem=recv,
            device_id={"depth": device},
            device_id_type=MESH,
        )

    def wave_copy(rnd, freq, part):
        lo, hi = parts[part]
        rows = pl.ds(lo, hi - lo)
        slot = rnd % wave_slots
        return remote(
            outbox.at[rnd, freq, rows],
            inbox.at[rnd, freq, rows],
            wave_send.at[slot, freq, part],
            wave_recv.at[slot, freq, part],
            ahead,
        )

    def share_copy(rnd, slot, lo, hi, step, count, device):
        rows = pl.ds(lo, hi - lo)
        return remote(
            share_out.at[rnd, pl.ds(step, count), rows],
            share_in.at[rnd, pl.ds(step, count), rows],
            share_send.at[slot],
            share_recv.at[slot],
            device,
        )

    def one_block(rnd, freq, b):
        lhs = jnp.concatenate([padded[freq, b + offs[k]] for k in range(band)], axis=1)
        rhs = jnp.concatenate(
            [
                jnp.concatenate([oper[freq, b, k, 0], oper[freq, b, k, 1]], axis=1)
                for k in range(band)
            ],
            axis=0,
        )
        both = jnp.dot(lhs, rhs, preferred_element_type=jnp.float32)
        re = [both[c * slots : (c + 1) * slots, :block] for c in range(nfield)]
        im = [both[c * slots : (c + 1) * slots, block:] for c in range(nfield)]
        new = [re[0] - im[1], im[0] + re[1], re[2] + im[3], re[3] - im[2]]
        rounded = jnp.concatenate(new, axis=0).astype(jnp.bfloat16)
        outbox[rnd, freq, b] = rounded
        wide = rounded.astype(jnp.float32)
        part = [wide[c * slots : (c + 1) * slots] for c in range(nfield)]
        image = part[0] * part[2] + part[1] * part[3]
        if freq > 0:
            image = image + half_image[b]
        if freq < freqs - 1:
            half_image[b] = image
        else:
            for slot in range(slots):
                slot_image[slot, pl.ds(b, 1), :] = image[slot : slot + 1] * scale

    def send_share(rnd, slot, lo, hi):
        for step in range(owners):
            share_out[rnd, step, lo:hi] = slot_image[slot_for((owner + step) % owners), lo:hi]
        for step in range(1, owners):
            share_copy(rnd, slot, lo, hi, step, 1, any_mate(step)).start()

    def finish_image(rnd, slot, lo, hi):
        share_copy(rnd, slot, lo, hi, 1, owners - 1, ahead).wait_recv()
        total = share_out[rnd, 0, lo:hi]
        for step in range(1, owners):
            total = total + share_in[rnd, step, lo:hi]
        images_ref[rnd, lo:hi] = total

    def drain_share(rnd, slot, lo, hi):
        share_copy(rnd, slot, lo, hi, 1, owners - 1, ahead).wait_send()

    def tail_slot(piece):
        return final % share_slots if piece == 0 else share_slots + piece - 1

    @pl.loop(0, HANDOVERS)
    def _(rnd):
        for freq in range(freqs):
            closing = freq == freqs - 1
            have = 0
            sent = 0
            shared = 0
            for group, (lo, hi) in enumerate(groups):
                need = min(hi + reach, nblk)
                fresh = []
                while have < len(parts) and (parts[have][0] < need):
                    fresh.append(have)
                    have += 1

                @pl.when(rnd == 0)
                def _():
                    if group == 0:
                        unpack_front(freq)
                    load(freq, group).wait()
                    for ahead_of in queue[freq * len(groups) + group :][DEEP : DEEP + 1]:
                        load(*ahead_of).start()

                @pl.when(rnd > 0)
                def _():
                    for part in fresh:
                        start, end = parts[part]
                        wave_copy(rnd - 1, freq, part).wait_recv()
                        padded[freq, reach + start : reach + end] = inbox[
                            rnd - 1, freq, start:end
                        ]

                for b in range(lo, hi):
                    one_block(rnd, freq, b)

                if freq == 0 and group == 0:

                    @pl.when(rnd == 0)
                    def _():
                        pl.semaphore_wait(barrier, len(greeted))

                outgoing = []
                while sent < len(parts) and parts[sent][1] <= hi:
                    outgoing.append(sent)
                    sent += 1

                if outgoing:

                    @pl.when((rnd >= wave_slots) & (rnd < final))
                    def _():
                        for part in outgoing:
                            wave_copy(rnd - wave_slots, freq, part).wait_send()

                    @pl.when(rnd < final)
                    def _():
                        for part in outgoing:
                            wave_copy(rnd, freq, part).start()

                @pl.when(rnd == final)
                def _():
                    nonlocal shared
                    while closing and shared < len(tails) and tails[shared][1] <= hi:
                        send_share(rnd, tail_slot(shared), *tails[shared])
                        shared += 1
                    for b in range(lo, hi):
                        cols = slice(b * block, (b + 1) * block)
                        for c in range(nfield):
                            rows = slice(c * slots, (c + 1) * slots)
                            last_ref[c, freq, :, cols] = outbox[rnd, freq, b, rows, :]

            if freq == 0:

                @pl.when(rnd >= LAG)
                def _():
                    before = rnd - LAG
                    finish_image(before, before % share_slots, 0, nblk)
                    drain_share(before, before % share_slots, 0, nblk)

        @pl.when(rnd < final)
        def _():
            send_share(rnd, rnd % share_slots, 0, nblk)

    for rnd in range(max(final - wave_slots, 0), final):
        for freq in range(freqs):
            for part in range(len(parts)):
                wave_copy(rnd, freq, part).wait_send()
    for rnd in range(max(HANDOVERS - LAG, 0), final):
        finish_image(rnd, rnd % share_slots, 0, nblk)
        drain_share(rnd, rnd % share_slots, 0, nblk)
    for piece, (lo, hi) in enumerate(tails):
        finish_image(final, tail_slot(piece), lo, hi)
    for piece, (lo, hi) in enumerate(tails):
        drain_share(final, tail_slot(piece), lo, hi)


def store(images_ref, last_ref, images_hbm, last_hbm, sem):
    copies = [
        pltpu.make_async_copy(last_ref, last_hbm, sem.at[0]),
        pltpu.make_async_copy(images_ref, images_hbm, sem.at[1]),
    ]
    for copy in copies:
        copy.start()
    for copy in copies:
        copy.wait()


def on_device(sections, owners, fronts, extrap, offsets, assign):
    nfield, freqs, slots, points = fronts.shape
    _, nblk, band, _, block, _ = extrap.shape
    moves = HANDOVERS - 1
    wave = (moves, freqs, nblk, nfield * slots, block)
    share = (HANDOVERS, owners, nblk, block)
    wave_slots = min(2 if sections == 2 else moves, moves)
    groups, parts, tails = (len(cuts(nblk, e)) for e in (GROUP_ENDS, PART_ENDS, TAIL_ENDS))
    vmem = pl.BlockSpec(memory_space=pltpu.VMEM)
    hbm = pl.BlockSpec(memory_space=pltpu.HBM)
    dma = pltpu.SemaphoreType.DMA
    shapes = (
        jax.ShapeDtypeStruct((HANDOVERS, nblk, block), jnp.float32),
        jax.ShapeDtypeStruct(fronts.shape, fronts.dtype),
    )
    held = [
        pltpu.with_memory_space_constraint(a, pltpu.HBM) for a in (offsets, assign, fronts, extrap)
    ]
    images, last = pl.pallas_call(
        functools.partial(kernel, sections, owners),
        out_shape=shapes,
        in_specs=[hbm] * 4,
        out_specs=(vmem, vmem),
        scratch_shapes=[
            pltpu.SMEM(offsets.shape, offsets.dtype),
            pltpu.SMEM(assign.shape, assign.dtype),
            pltpu.VMEM(fronts.shape, fronts.dtype),
            pltpu.VMEM(extrap.shape, extrap.dtype),
            pltpu.VMEM((freqs, nblk + 2 * (band // 2), nfield * slots, block), fronts.dtype),
            pltpu.VMEM((HANDOVERS,) + wave[1:], fronts.dtype),
            pltpu.VMEM(wave, fronts.dtype),
            pltpu.VMEM((nblk, slots, block), jnp.float32),
            pltpu.VMEM((slots, nblk, block), jnp.float32),
            pltpu.VMEM(share, jnp.float32),
            pltpu.VMEM(share, jnp.float32),
            dma((2,)),
            dma((freqs,)),
            dma((freqs, groups)),
            dma((wave_slots, freqs, parts)),
            dma((wave_slots, freqs, parts)),
            dma((2 * LAG + tails - 1,)),
            dma((2 * LAG + tails - 1,)),
        ],
        compiler_params=pltpu.CompilerParams(
            collective_id=0, has_side_effects=True, vmem_limit_bytes=VMEM_BYTES
        ),
    )(*held)
    images, last = pl.pallas_call(
        store,
        out_shape=shapes,
        in_specs=[vmem, vmem],
        out_specs=(hbm, hbm),
        scratch_shapes=[dma((2,))],
        compiler_params=pltpu.CompilerParams(vmem_limit_bytes=STORE_BYTES),
    )(images, last)
    return images.reshape(HANDOVERS, slots // owners, points), last


def solution(mesh):
    depth = mesh.shape["depth"]

    def program(fronts, extrap, offsets, assign):
        sections = offsets.shape[0]
        placed = (
            P(None, ("groups", "depth"), None, None),
            P("depth", None, None, None, None, None),
            P(),
            P(),
        )
        return jax.shard_map(
            functools.partial(on_device, sections, depth // sections),
            mesh=mesh,
            in_specs=placed,
            out_specs=(
                P(None, ("groups", "depth"), None),
                P(None, ("groups", "depth"), None, None),
            ),
            check_vma=False,
        )(fronts, extrap, offsets, assign)

    return program
```

```python
import functools
import math

import jax
import jax.numpy as jnp
from jax import lax
from jax.experimental import pallas as pl
from jax.experimental.pallas import tpu as pltpu
from jax.sharding import PartitionSpec as P

HANDOVERS = 8
GROUP_ENDS = (4, 8, 12)
PART_ENDS = (4, 8, 12)
TAIL_ENDS = (8,)
LAG = 2
WHERE = 0
DEEP = 3
SENDS = 1
FIRST_ENDS = (1, 2)
VMEM_BYTES = 48 << 20
STORE_BYTES = 1 << 20
MESH = pl.DeviceIdType.MESH


def cuts(total, ends):
    edges = [0] + [e for e in ends if 0 < e < total] + [total]
    return list(zip(edges[:-1], edges[1:]))


def kernel(
    sections,
    owners,
    offsets_hbm,
    assign_hbm,
    fronts_hbm,
    extrap_hbm,
    images_ref,
    last_ref,
    offsets_ref,
    assign_ref,
    fronts_ref,
    oper,
    padded,
    outbox,
    inbox,
    half_image,
    slot_image,
    share_out,
    share_in,
    table_sem,
    front_sem,
    load_sem,
    wave_send,
    wave_recv,
    share_send,
    share_recv,
):
    nfield, freqs, slots, _ = fronts_ref.shape
    nblk, band, block = oper.shape[1], oper.shape[2], oper.shape[-1]
    reach = band // 2
    scale = 1.0 / math.sqrt(2.0 * freqs * owners)
    final = HANDOVERS - 1
    me = lax.axis_index("depth")
    depth = sections * owners
    section = me // owners
    owner = me % owners
    ahead = (me + owners) % depth
    behind = (me + depth - owners) % depth

    groups = cuts(nblk, GROUP_ENDS)
    parts = cuts(nblk, PART_ENDS)
    tails = cuts(nblk, TAIL_ENDS)
    load_slots = load_sem.shape[0]
    send_slots, wave_slots = wave_send.shape[0], wave_recv.shape[0]
    share_slots = 2 * LAG

    def any_mate(step):
        return section * owners + (owner + step) % owners

    barrier = pltpu.get_barrier_semaphore()
    greeted = [ahead] + ([behind] if sections > 2 else [])
    greeted = greeted + [any_mate(d) for d in range(1, owners)]
    for device in greeted:
        pl.semaphore_signal(barrier, inc=1, device_id={"depth": device}, device_id_type=MESH)

    offsets_load = pltpu.make_async_copy(offsets_hbm, offsets_ref, table_sem.at[0])
    assign_load = pltpu.make_async_copy(assign_hbm, assign_ref, table_sem.at[1])

    def front_load(freq):
        return pltpu.make_async_copy(
            fronts_hbm.at[:, freq], fronts_ref.at[:, freq], front_sem.at[freq]
        )

    first = cuts(groups[0][1], FIRST_ENDS)
    queue = [(0, lo, hi) for lo, hi in first] + [(0, lo, hi) for lo, hi in groups[1:]]
    queue += [(freq, lo, hi) for freq in range(1, freqs) for lo, hi in groups]

    def load(place):
        freq, lo, hi = queue[place]
        rows = pl.ds(lo, hi - lo)
        return pltpu.make_async_copy(
            extrap_hbm.at[freq, rows], oper.at[freq, rows], load_sem.at[place % load_slots]
        )

    def take(freq, lo, hi):
        place = queue.index((freq, lo, hi))
        load(place).wait()
        if place + load_slots < len(queue):
            load(place + load_slots).start()

    offsets_load.start()
    front_load(0).start()
    for place in range(min(load_slots, len(queue))):
        load(place).start()
    assign_load.start()
    for freq in range(1, freqs):
        front_load(freq).start()

    blank = jnp.zeros((reach,) + padded.shape[2:], padded.dtype)
    for freq in range(freqs):
        padded[freq, 0:reach] = blank
        padded[freq, reach + nblk : 2 * reach + nblk] = blank

    offsets_load.wait()
    offs = [offsets_ref[section, k] + reach for k in range(band)]

    def slot_for(target):
        chosen = jnp.int32(0)
        for slot in range(slots):
            chosen = jnp.where(assign_ref[section, slot] == target, slot, chosen)
        return chosen

    def unpack_front(freq):
        front_load(freq).wait()
        for b in range(nblk):
            cols = slice(b * block, (b + 1) * block)
            rows = [fronts_ref[c, freq, :, cols].astype(jnp.float32) for c in range(nfield)]
            padded[freq, reach + b] = jnp.concatenate(rows, axis=0).astype(padded.dtype)

    def remote(src, dst, send, recv, device):
        return pltpu.make_async_remote_copy(
            src_ref=src,
            dst_ref=dst,
            send_sem=send,
            recv_sem=recv,
            device_id={"depth": device},
            device_id_type=MESH,
        )

    def wave_copy(rnd, freq, part, some=None):
        lo, hi = some or parts[part]
        rows = pl.ds(lo, hi - lo)
        return remote(
            outbox.at[rnd, freq, rows],
            inbox.at[rnd, freq, rows],
            wave_send.at[rnd % send_slots, freq, part],
            wave_recv.at[rnd % wave_slots, freq, part],
            ahead,
        )

    def share_copy(rnd, slot, lo, hi, step, count, device):
        rows = pl.ds(lo, hi - lo)
        return remote(
            share_out.at[rnd, pl.ds(step, count), rows],
            share_in.at[rnd, pl.ds(step, count), rows],
            share_send.at[slot],
            share_recv.at[slot],
            device,
        )

    def one_block(rnd, freq, b):
        lhs = jnp.concatenate([padded[freq, b + offs[k]] for k in range(band)], axis=1)
        rhs = jnp.concatenate(
            [
                jnp.concatenate([oper[freq, b, k, 0], oper[freq, b, k, 1]], axis=1)
                for k in range(band)
            ],
            axis=0,
        )
        both = jnp.dot(lhs, rhs, preferred_element_type=jnp.float32)
        re = [both[c * slots : (c + 1) * slots, :block] for c in range(nfield)]
        im = [both[c * slots : (c + 1) * slots, block:] for c in range(nfield)]
        new = [re[0] - im[1], im[0] + re[1], re[2] + im[3], re[3] - im[2]]
        rounded = jnp.concatenate(new, axis=0).astype(jnp.bfloat16)
        outbox[rnd, freq, b] = rounded
        wide = rounded.astype(jnp.float32)
        part = [wide[c * slots : (c + 1) * slots] for c in range(nfield)]
        image = part[0] * part[2] + part[1] * part[3]
        if freq > 0:
            image = image + half_image[b]
        if freq < freqs - 1:
            half_image[b] = image
        else:
            for slot in range(slots):
                slot_image[slot, pl.ds(b, 1), :] = image[slot : slot + 1] * scale

    def send_share(rnd, slot, lo, hi):
        for step in range(owners):
            share_out[rnd, step, lo:hi] = slot_image[slot_for((owner + step) % owners), lo:hi]
        for step in range(1, owners):
            share_copy(rnd, slot, lo, hi, step, 1, any_mate(step)).start()

    def finish_image(rnd, slot, lo, hi):
        share_copy(rnd, slot, lo, hi, 1, owners - 1, ahead).wait_recv()
        total = share_out[rnd, 0, lo:hi]
        for step in range(1, owners):
            total = total + share_in[rnd, step, lo:hi]
        images_ref[rnd, lo:hi] = total

    def drain_share(rnd, slot, lo, hi):
        share_copy(rnd, slot, lo, hi, 1, owners - 1, ahead).wait_send()

    def tail_slot(piece):
        return final % share_slots if piece == 0 else share_slots + piece - 1

    @pl.loop(0, HANDOVERS)
    def _(rnd):
        for freq in range(freqs):
            closing = freq == freqs - 1
            have = 0
            sent = 0
            shared = 0
            for group, (lo, hi) in enumerate(groups):
                need = min(hi + reach, nblk)
                fresh = []
                while have < len(parts) and (parts[have][0] < need):
                    fresh.append(have)
                    have += 1

                opening = freq == 0 and group == 0

                @pl.when(rnd == 0)
                def _():
                    if group == 0:
                        unpack_front(freq)
                    if not opening:
                        take(freq, lo, hi)

                @pl.when(rnd > 0)
                def _():
                    for part in fresh:
                        start, end = parts[part]
                        wave_copy(rnd - 1, freq, part).wait_recv()
                        padded[freq, reach + start : reach + end] = inbox[
                            rnd - 1, freq, start:end
                        ]

                for start, end in first if opening else [(lo, hi)]:
                    if opening:

                        @pl.when(rnd == 0)
                        def _():
                            take(freq, start, end)

                    for b in range(start, end):
                        one_block(rnd, freq, b)

                    if opening:

                        @pl.when(rnd == 0)
                        def _():
                            if start == 0:
                                pl.semaphore_wait(barrier, len(greeted))
                                assign_load.wait()
                            wave_copy(rnd, freq, 0, (start, end)).start()

                outgoing = []
                while sent < len(parts) and parts[sent][1] <= hi:
                    outgoing.append(sent)
                    sent += 1

                if outgoing:

                    @pl.when((rnd >= send_slots) & (rnd < final))
                    def _():
                        for part in outgoing:
                            wave_copy(rnd - send_slots, freq, part).wait_send()

                    @pl.when((rnd >= int(opening)) & (rnd < final))
                    def _():
                        for part in outgoing:
                            wave_copy(rnd, freq, part).start()

                @pl.when(rnd == final)
                def _():
                    nonlocal shared
                    while closing and shared < len(tails) and tails[shared][1] <= hi:
                        send_share(rnd, tail_slot(shared), *tails[shared])
                        shared += 1
                    for b in range(lo, hi):
                        cols = slice(b * block, (b + 1) * block)
                        for c in range(nfield):
                            rows = slice(c * slots, (c + 1) * slots)
                            last_ref[c, freq, :, cols] = outbox[rnd, freq, b, rows, :]

            if freq == WHERE:

                @pl.when(rnd >= LAG)
                def _():
                    before = rnd - LAG
                    finish_image(before, before % share_slots, 0, nblk)
                    drain_share(before, before % share_slots, 0, nblk)

        @pl.when(rnd < final)
        def _():
            send_share(rnd, rnd % share_slots, 0, nblk)

    for rnd in range(max(final - send_slots, 0), final):
        for freq in range(freqs):
            for part in range(len(parts)):
                wave_copy(rnd, freq, part).wait_send()
    for rnd in range(max(HANDOVERS - LAG, 0), final):
        finish_image(rnd, rnd % share_slots, 0, nblk)
        drain_share(rnd, rnd % share_slots, 0, nblk)
    for piece, (lo, hi) in enumerate(tails):
        finish_image(final, tail_slot(piece), lo, hi)
    for piece, (lo, hi) in enumerate(tails):
        drain_share(final, tail_slot(piece), lo, hi)


def store(images_ref, last_ref, images_hbm, last_hbm, sem):
    copies = [
        pltpu.make_async_copy(last_ref, last_hbm, sem.at[0]),
        pltpu.make_async_copy(images_ref, images_hbm, sem.at[1]),
    ]
    for copy in copies:
        copy.start()
    for copy in copies:
        copy.wait()


def on_device(sections, owners, fronts, extrap, offsets, assign):
    nfield, freqs, slots, points = fronts.shape
    _, nblk, band, _, block, _ = extrap.shape
    moves = HANDOVERS - 1
    wave = (moves, freqs, nblk, nfield * slots, block)
    share = (HANDOVERS, owners, nblk, block)
    wave_slots = min(2 if sections == 2 else moves, moves)
    send_slots = SENDS or wave_slots
    parts, tails = (len(cuts(nblk, e)) for e in (PART_ENDS, TAIL_ENDS))
    vmem = pl.BlockSpec(memory_space=pltpu.VMEM)
    hbm = pl.BlockSpec(memory_space=pltpu.HBM)
    dma = pltpu.SemaphoreType.DMA
    shapes = (
        jax.ShapeDtypeStruct((HANDOVERS, nblk, block), jnp.float32),
        jax.ShapeDtypeStruct(fronts.shape, fronts.dtype),
    )
    held = [
        pltpu.with_memory_space_constraint(a, pltpu.HBM) for a in (offsets, assign, fronts, extrap)
    ]
    images, last = pl.pallas_call(
        functools.partial(kernel, sections, owners),
        out_shape=shapes,
        in_specs=[hbm] * 4,
        out_specs=(vmem, vmem),
        scratch_shapes=[
            pltpu.SMEM(offsets.shape, offsets.dtype),
            pltpu.SMEM(assign.shape, assign.dtype),
            pltpu.VMEM(fronts.shape, fronts.dtype),
            pltpu.VMEM(extrap.shape, extrap.dtype),
            pltpu.VMEM((freqs, nblk + 2 * (band // 2), nfield * slots, block), fronts.dtype),
            pltpu.VMEM((HANDOVERS,) + wave[1:], fronts.dtype),
            pltpu.VMEM(wave, fronts.dtype),
            pltpu.VMEM((nblk, slots, block), jnp.float32),
            pltpu.VMEM((slots, nblk, block), jnp.float32),
            pltpu.VMEM(share, jnp.float32),
            pltpu.VMEM(share, jnp.float32),
            dma((2,)),
            dma((freqs,)),
            dma((DEEP,)),
            dma((send_slots, freqs, parts)),
            dma((wave_slots, freqs, parts)),
            dma((2 * LAG + tails - 1,)),
            dma((2 * LAG + tails - 1,)),
        ],
        compiler_params=pltpu.CompilerParams(
            collective_id=0, has_side_effects=True, vmem_limit_bytes=VMEM_BYTES
        ),
    )(*held)
    images, last = pl.pallas_call(
        store,
        out_shape=shapes,
        in_specs=[vmem, vmem],
        out_specs=(hbm, hbm),
        scratch_shapes=[dma((2,))],
        compiler_params=pltpu.CompilerParams(vmem_limit_bytes=STORE_BYTES),
    )(images, last)
    return images.reshape(HANDOVERS, slots // owners, points), last


def solution(mesh):
    depth = mesh.shape["depth"]

    def program(fronts, extrap, offsets, assign):
        sections = offsets.shape[0]
        placed = (
            P(None, ("groups", "depth"), None, None),
            P("depth", None, None, None, None, None),
            P(),
            P(),
        )
        return jax.shard_map(
            functools.partial(on_device, sections, depth // sections),
            mesh=mesh,
            in_specs=placed,
            out_specs=(
                P(None, ("groups", "depth"), None),
                P(None, ("groups", "depth"), None, None),
            ),
            check_vma=False,
        )(fronts, extrap, offsets, assign)

    return program
```

```python
import functools
import math

import jax
import jax.numpy as jnp
from jax import lax
from jax.experimental import pallas as pl
from jax.experimental.pallas import tpu as pltpu
from jax.sharding import PartitionSpec as P

HANDOVERS = 8
GROUP_ENDS = (4, 8, 10, 12)
PART_ENDS = (4, 8, 12)
TAIL_ENDS = (8,)
LAG = 2
WHERE = 0
DEEP = 3
SENDS = 1
FIRST_ENDS = (1, 2)
VMEM_BYTES = 48 << 20
STORE_BYTES = 1 << 20
MESH = pl.DeviceIdType.MESH


def cuts(total, ends):
    edges = [0] + [e for e in ends if 0 < e < total] + [total]
    return list(zip(edges[:-1], edges[1:]))


def kernel(
    sections,
    owners,
    offsets_hbm,
    assign_hbm,
    fronts_hbm,
    extrap_hbm,
    images_ref,
    last_ref,
    offsets_ref,
    assign_ref,
    fronts_ref,
    oper,
    padded,
    outbox,
    inbox,
    half_image,
    slot_image,
    share_out,
    share_in,
    table_sem,
    front_sem,
    load_sem,
    wave_send,
    wave_recv,
    share_send,
    share_recv,
):
    nfield, freqs, slots, _ = fronts_ref.shape
    nblk, band, block = oper.shape[1], oper.shape[2], oper.shape[-1]
    reach = band // 2
    scale = 1.0 / math.sqrt(2.0 * freqs * owners)
    final = HANDOVERS - 1
    me = lax.axis_index("depth")
    depth = sections * owners
    section = me // owners
    owner = me % owners
    ahead = (me + owners) % depth
    behind = (me + depth - owners) % depth

    groups = cuts(nblk, GROUP_ENDS)
    parts = cuts(nblk, PART_ENDS)
    tails = cuts(nblk, TAIL_ENDS)
    load_slots = load_sem.shape[0]
    send_slots, wave_slots = wave_send.shape[0], wave_recv.shape[0]
    share_slots = 2 * LAG

    def any_mate(step):
        return section * owners + (owner + step) % owners

    barrier = pltpu.get_barrier_semaphore()
    greeted = [ahead] + ([behind] if sections > 2 else [])
    greeted = greeted + [any_mate(d) for d in range(1, owners)]
    for device in greeted:
        pl.semaphore_signal(barrier, inc=1, device_id={"depth": device}, device_id_type=MESH)

    offsets_load = pltpu.make_async_copy(offsets_hbm, offsets_ref, table_sem.at[0])
    assign_load = pltpu.make_async_copy(assign_hbm, assign_ref, table_sem.at[1])

    def front_load(freq):
        return pltpu.make_async_copy(
            fronts_hbm.at[:, freq], fronts_ref.at[:, freq], front_sem.at[freq]
        )

    first = cuts(groups[0][1], FIRST_ENDS)
    queue = [(0, lo, hi) for lo, hi in first] + [(0, lo, hi) for lo, hi in groups[1:]]
    queue += [(freq, lo, hi) for freq in range(1, freqs) for lo, hi in groups]

    def load(place):
        freq, lo, hi = queue[place]
        rows = pl.ds(lo, hi - lo)
        return pltpu.make_async_copy(
            extrap_hbm.at[freq, rows], oper.at[freq, rows], load_sem.at[place % load_slots]
        )

    def take(freq, lo, hi):
        place = queue.index((freq, lo, hi))
        load(place).wait()
        if place + load_slots < len(queue):
            load(place + load_slots).start()

    offsets_load.start()
    front_load(0).start()
    for place in range(min(load_slots, len(queue))):
        load(place).start()
    assign_load.start()
    for freq in range(1, freqs):
        front_load(freq).start()

    blank = jnp.zeros((reach,) + padded.shape[2:], padded.dtype)
    for freq in range(freqs):
        padded[freq, 0:reach] = blank
        padded[freq, reach + nblk : 2 * reach + nblk] = blank

    offsets_load.wait()
    offs = [offsets_ref[section, k] + reach for k in range(band)]

    def slot_for(target):
        chosen = jnp.int32(0)
        for slot in range(slots):
            chosen = jnp.where(assign_ref[section, slot] == target, slot, chosen)
        return chosen

    def unpack_front(freq):
        front_load(freq).wait()
        for b in range(nblk):
            cols = slice(b * block, (b + 1) * block)
            rows = [fronts_ref[c, freq, :, cols].astype(jnp.float32) for c in range(nfield)]
            padded[freq, reach + b] = jnp.concatenate(rows, axis=0).astype(padded.dtype)

    def remote(src, dst, send, recv, device):
        return pltpu.make_async_remote_copy(
            src_ref=src,
            dst_ref=dst,
            send_sem=send,
            recv_sem=recv,
            device_id={"depth": device},
            device_id_type=MESH,
        )

    def wave_copy(rnd, freq, part, some=None):
        lo, hi = some or parts[part]
        rows = pl.ds(lo, hi - lo)
        return remote(
            outbox.at[rnd, freq, rows],
            inbox.at[rnd, freq, rows],
            wave_send.at[rnd % send_slots, freq, part],
            wave_recv.at[rnd % wave_slots, freq, part],
            ahead,
        )

    def share_copy(rnd, slot, lo, hi, step, count, device):
        rows = pl.ds(lo, hi - lo)
        return remote(
            share_out.at[rnd, pl.ds(step, count), rows],
            share_in.at[rnd, pl.ds(step, count), rows],
            share_send.at[slot],
            share_recv.at[slot],
            device,
        )

    def one_block(rnd, freq, b):
        lhs = jnp.concatenate([padded[freq, b + offs[k]] for k in range(band)], axis=1)
        rhs = jnp.concatenate(
            [
                jnp.concatenate([oper[freq, b, k, 0], oper[freq, b, k, 1]], axis=1)
                for k in range(band)
            ],
            axis=0,
        )
        both = jnp.dot(lhs, rhs, preferred_element_type=jnp.float32)
        re = [both[c * slots : (c + 1) * slots, :block] for c in range(nfield)]
        im = [both[c * slots : (c + 1) * slots, block:] for c in range(nfield)]
        new = [re[0] - im[1], im[0] + re[1], re[2] + im[3], re[3] - im[2]]
        rounded = jnp.concatenate(new, axis=0).astype(jnp.bfloat16)
        outbox[rnd, freq, b] = rounded
        wide = rounded.astype(jnp.float32)
        part = [wide[c * slots : (c + 1) * slots] for c in range(nfield)]
        image = part[0] * part[2] + part[1] * part[3]
        if freq > 0:
            image = image + half_image[b]
        if freq < freqs - 1:
            half_image[b] = image
        else:
            for slot in range(slots):
                slot_image[slot, pl.ds(b, 1), :] = image[slot : slot + 1] * scale

    def send_share(rnd, slot, lo, hi):
        for step in range(owners):
            share_out[rnd, step, lo:hi] = slot_image[slot_for((owner + step) % owners), lo:hi]
        for step in range(1, owners):
            share_copy(rnd, slot, lo, hi, step, 1, any_mate(step)).start()

    def finish_image(rnd, slot, lo, hi):
        share_copy(rnd, slot, lo, hi, 1, owners - 1, ahead).wait_recv()
        total = share_out[rnd, 0, lo:hi]
        for step in range(1, owners):
            total = total + share_in[rnd, step, lo:hi]
        images_ref[rnd, lo:hi] = total

    def drain_share(rnd, slot, lo, hi):
        share_copy(rnd, slot, lo, hi, 1, owners - 1, ahead).wait_send()

    def tail_slot(piece):
        return final % share_slots if piece == 0 else share_slots + piece - 1

    @pl.loop(0, HANDOVERS)
    def _(rnd):
        for freq in range(freqs):
            closing = freq == freqs - 1
            have = 0
            sent = 0
            shared = 0
            for group, (lo, hi) in enumerate(groups):
                need = min(hi + reach, nblk)
                fresh = []
                while have < len(parts) and (parts[have][0] < need):
                    fresh.append(have)
                    have += 1

                opening = freq == 0 and group == 0

                @pl.when(rnd == 0)
                def _():
                    if group == 0:
                        unpack_front(freq)
                    if not opening:
                        take(freq, lo, hi)

                @pl.when(rnd > 0)
                def _():
                    for part in fresh:
                        start, end = parts[part]
                        wave_copy(rnd - 1, freq, part).wait_recv()
                        padded[freq, reach + start : reach + end] = inbox[
                            rnd - 1, freq, start:end
                        ]

                for start, end in first if opening else [(lo, hi)]:
                    if opening:

                        @pl.when(rnd == 0)
                        def _():
                            take(freq, start, end)

                    for b in range(start, end):
                        one_block(rnd, freq, b)

                    if opening:

                        @pl.when(rnd == 0)
                        def _():
                            if start == 0:
                                pl.semaphore_wait(barrier, len(greeted))
                                assign_load.wait()
                            wave_copy(rnd, freq, 0, (start, end)).start()

                outgoing = []
                while sent < len(parts) and parts[sent][1] <= hi:
                    outgoing.append(sent)
                    sent += 1

                if outgoing:

                    @pl.when((rnd >= send_slots) & (rnd < final))
                    def _():
                        for part in outgoing:
                            wave_copy(rnd - send_slots, freq, part).wait_send()

                    @pl.when((rnd >= int(opening)) & (rnd < final))
                    def _():
                        for part in outgoing:
                            wave_copy(rnd, freq, part).start()

                @pl.when(rnd == final)
                def _():
                    nonlocal shared
                    while closing and shared < len(tails) and tails[shared][1] <= hi:
                        send_share(rnd, tail_slot(shared), *tails[shared])
                        shared += 1
                    for b in range(lo, hi):
                        cols = slice(b * block, (b + 1) * block)
                        for c in range(nfield):
                            rows = slice(c * slots, (c + 1) * slots)
                            last_ref[c, freq, :, cols] = outbox[rnd, freq, b, rows, :]

            if freq == WHERE:

                @pl.when(rnd >= LAG)
                def _():
                    before = rnd - LAG
                    finish_image(before, before % share_slots, 0, nblk)
                    drain_share(before, before % share_slots, 0, nblk)

        @pl.when(rnd < final)
        def _():
            send_share(rnd, rnd % share_slots, 0, nblk)

    for rnd in range(max(final - send_slots, 0), final):
        for freq in range(freqs):
            for part in range(len(parts)):
                wave_copy(rnd, freq, part).wait_send()
    for rnd in range(max(HANDOVERS - LAG, 0), final):
        finish_image(rnd, rnd % share_slots, 0, nblk)
        drain_share(rnd, rnd % share_slots, 0, nblk)
    for piece, (lo, hi) in enumerate(tails):
        finish_image(final, tail_slot(piece), lo, hi)
    for piece, (lo, hi) in enumerate(tails):
        drain_share(final, tail_slot(piece), lo, hi)


def store(images_ref, last_ref, images_hbm, last_hbm, sem):
    copies = [
        pltpu.make_async_copy(last_ref, last_hbm, sem.at[0]),
        pltpu.make_async_copy(images_ref, images_hbm, sem.at[1]),
    ]
    for copy in copies:
        copy.start()
    for copy in copies:
        copy.wait()


def on_device(sections, owners, fronts, extrap, offsets, assign):
    nfield, freqs, slots, points = fronts.shape
    _, nblk, band, _, block, _ = extrap.shape
    moves = HANDOVERS - 1
    wave = (moves, freqs, nblk, nfield * slots, block)
    share = (HANDOVERS, owners, nblk, block)
    wave_slots = min(2 if sections == 2 else moves, moves)
    send_slots = SENDS or wave_slots
    parts, tails = (len(cuts(nblk, e)) for e in (PART_ENDS, TAIL_ENDS))
    vmem = pl.BlockSpec(memory_space=pltpu.VMEM)
    hbm = pl.BlockSpec(memory_space=pltpu.HBM)
    dma = pltpu.SemaphoreType.DMA
    shapes = (
        jax.ShapeDtypeStruct((HANDOVERS, nblk, block), jnp.float32),
        jax.ShapeDtypeStruct(fronts.shape, fronts.dtype),
    )
    held = [
        pltpu.with_memory_space_constraint(a, pltpu.HBM) for a in (offsets, assign, fronts, extrap)
    ]
    images, last = pl.pallas_call(
        functools.partial(kernel, sections, owners),
        out_shape=shapes,
        in_specs=[hbm] * 4,
        out_specs=(vmem, vmem),
        scratch_shapes=[
            pltpu.SMEM(offsets.shape, offsets.dtype),
            pltpu.SMEM(assign.shape, assign.dtype),
            pltpu.VMEM(fronts.shape, fronts.dtype),
            pltpu.VMEM(extrap.shape, extrap.dtype),
            pltpu.VMEM((freqs, nblk + 2 * (band // 2), nfield * slots, block), fronts.dtype),
            pltpu.VMEM((HANDOVERS,) + wave[1:], fronts.dtype),
            pltpu.VMEM(wave, fronts.dtype),
            pltpu.VMEM((nblk, slots, block), jnp.float32),
            pltpu.VMEM((slots, nblk, block), jnp.float32),
            pltpu.VMEM(share, jnp.float32),
            pltpu.VMEM(share, jnp.float32),
            dma((2,)),
            dma((freqs,)),
            dma((DEEP,)),
            dma((send_slots, freqs, parts)),
            dma((wave_slots, freqs, parts)),
            dma((2 * LAG + tails - 1,)),
            dma((2 * LAG + tails - 1,)),
        ],
        compiler_params=pltpu.CompilerParams(
            collective_id=0, has_side_effects=True, vmem_limit_bytes=VMEM_BYTES
        ),
    )(*held)
    images, last = pl.pallas_call(
        store,
        out_shape=shapes,
        in_specs=[vmem, vmem],
        out_specs=(hbm, hbm),
        scratch_shapes=[dma((2,))],
        compiler_params=pltpu.CompilerParams(vmem_limit_bytes=STORE_BYTES),
    )(images, last)
    return images.reshape(HANDOVERS, slots // owners, points), last


def solution(mesh):
    depth = mesh.shape["depth"]

    def program(fronts, extrap, offsets, assign):
        sections = offsets.shape[0]
        placed = (
            P(None, ("groups", "depth"), None, None),
            P("depth", None, None, None, None, None),
            P(),
            P(),
        )
        return jax.shard_map(
            functools.partial(on_device, sections, depth // sections),
            mesh=mesh,
            in_specs=placed,
            out_specs=(
                P(None, ("groups", "depth"), None),
                P(None, ("groups", "depth"), None, None),
            ),
            check_vma=False,
        )(fronts, extrap, offsets, assign)

    return program
```

```python
import functools
import math

import jax
import jax.numpy as jnp
from jax import lax
from jax.experimental import pallas as pl
from jax.experimental.pallas import tpu as pltpu
from jax.sharding import PartitionSpec as P

HANDOVERS = 8
GROUP_ENDS = (4, 8, 10, 12)
PART_ENDS = (4, 8, 12)
TAIL_ENDS = ()
LAG = 2
WHERE = 0
DEEP = 3
SENDS = 1
FIRST_ENDS = (1, 2)
VMEM_BYTES = 48 << 20
STORE_BYTES = 1 << 20
MESH = pl.DeviceIdType.MESH


def cuts(total, ends):
    edges = [0] + [e for e in ends if 0 < e < total] + [total]
    return list(zip(edges[:-1], edges[1:]))


def kernel(
    sections,
    owners,
    offsets_hbm,
    assign_hbm,
    fronts_hbm,
    extrap_hbm,
    images_ref,
    last_ref,
    offsets_ref,
    assign_ref,
    fronts_ref,
    oper,
    padded,
    outbox,
    inbox,
    half_image,
    slot_image,
    share_out,
    share_in,
    table_sem,
    front_sem,
    load_sem,
    wave_send,
    wave_recv,
    share_send,
    share_recv,
):
    nfield, freqs, slots, _ = fronts_ref.shape
    nblk, band, block = oper.shape[1], oper.shape[2], oper.shape[-1]
    reach = band // 2
    scale = 1.0 / math.sqrt(2.0 * freqs * owners)
    final = HANDOVERS - 1
    me = lax.axis_index("depth")
    depth = sections * owners
    section = me // owners
    owner = me % owners
    ahead = (me + owners) % depth
    behind = (me + depth - owners) % depth

    groups = cuts(nblk, GROUP_ENDS)
    parts = cuts(nblk, PART_ENDS)
    tails = cuts(nblk, TAIL_ENDS)
    load_slots = load_sem.shape[0]
    send_slots, wave_slots = wave_send.shape[0], wave_recv.shape[0]
    share_slots = 2 * LAG

    def any_mate(step):
        return section * owners + (owner + step) % owners

    barrier = pltpu.get_barrier_semaphore()
    greeted = [ahead] + ([behind] if sections > 2 else [])
    greeted = greeted + [any_mate(d) for d in range(1, owners)]
    for device in greeted:
        pl.semaphore_signal(barrier, inc=1, device_id={"depth": device}, device_id_type=MESH)

    offsets_load = pltpu.make_async_copy(offsets_hbm, offsets_ref, table_sem.at[0])
    assign_load = pltpu.make_async_copy(assign_hbm, assign_ref, table_sem.at[1])

    def front_load(freq):
        return pltpu.make_async_copy(
            fronts_hbm.at[:, freq], fronts_ref.at[:, freq], front_sem.at[freq]
        )

    first = cuts(groups[0][1], FIRST_ENDS)
    queue = [(0, lo, hi) for lo, hi in first] + [(0, lo, hi) for lo, hi in groups[1:]]
    queue += [(freq, lo, hi) for freq in range(1, freqs) for lo, hi in groups]

    def load(place):
        freq, lo, hi = queue[place]
        rows = pl.ds(lo, hi - lo)
        return pltpu.make_async_copy(
            extrap_hbm.at[freq, rows], oper.at[freq, rows], load_sem.at[place % load_slots]
        )

    def take(freq, lo, hi):
        place = queue.index((freq, lo, hi))
        load(place).wait()
        if place + load_slots < len(queue):
            load(place + load_slots).start()

    offsets_load.start()
    front_load(0).start()
    for place in range(min(load_slots, len(queue))):
        load(place).start()
    assign_load.start()
    for freq in range(1, freqs):
        front_load(freq).start()

    blank = jnp.zeros((reach,) + padded.shape[2:], padded.dtype)
    for freq in range(freqs):
        padded[freq, 0:reach] = blank
        padded[freq, reach + nblk : 2 * reach + nblk] = blank

    offsets_load.wait()
    offs = [offsets_ref[section, k] + reach for k in range(band)]

    def slot_for(target):
        chosen = jnp.int32(0)
        for slot in range(slots):
            chosen = jnp.where(assign_ref[section, slot] == target, slot, chosen)
        return chosen

    def unpack_front(freq):
        front_load(freq).wait()
        for b in range(nblk):
            cols = slice(b * block, (b + 1) * block)
            rows = [fronts_ref[c, freq, :, cols].astype(jnp.float32) for c in range(nfield)]
            padded[freq, reach + b] = jnp.concatenate(rows, axis=0).astype(padded.dtype)

    def remote(src, dst, send, recv, device):
        return pltpu.make_async_remote_copy(
            src_ref=src,
            dst_ref=dst,
            send_sem=send,
            recv_sem=recv,
            device_id={"depth": device},
            device_id_type=MESH,
        )

    def wave_copy(rnd, freq, part, some=None):
        lo, hi = some or parts[part]
        rows = pl.ds(lo, hi - lo)
        return remote(
            outbox.at[rnd, freq, rows],
            inbox.at[rnd, freq, rows],
            wave_send.at[rnd % send_slots, freq, part],
            wave_recv.at[rnd % wave_slots, freq, part],
            ahead,
        )

    def share_copy(rnd, slot, lo, hi, step, count, device):
        rows = pl.ds(lo, hi - lo)
        return remote(
            share_out.at[rnd, pl.ds(step, count), rows],
            share_in.at[rnd, pl.ds(step, count), rows],
            share_send.at[slot],
            share_recv.at[slot],
            device,
        )

    def one_block(rnd, freq, b):
        lhs = jnp.concatenate([padded[freq, b + offs[k]] for k in range(band)], axis=1)
        rhs = jnp.concatenate(
            [
                jnp.concatenate([oper[freq, b, k, 0], oper[freq, b, k, 1]], axis=1)
                for k in range(band)
            ],
            axis=0,
        )
        both = jnp.dot(lhs, rhs, preferred_element_type=jnp.float32)
        re = [both[c * slots : (c + 1) * slots, :block] for c in range(nfield)]
        im = [both[c * slots : (c + 1) * slots, block:] for c in range(nfield)]
        new = [re[0] - im[1], im[0] + re[1], re[2] + im[3], re[3] - im[2]]
        rounded = jnp.concatenate(new, axis=0).astype(jnp.bfloat16)
        outbox[rnd, freq, b] = rounded
        wide = rounded.astype(jnp.float32)
        part = [wide[c * slots : (c + 1) * slots] for c in range(nfield)]
        image = part[0] * part[2] + part[1] * part[3]
        if freq > 0:
            image = image + half_image[b]
        if freq < freqs - 1:
            half_image[b] = image
        else:
            for slot in range(slots):
                slot_image[slot, pl.ds(b, 1), :] = image[slot : slot + 1] * scale

    def send_share(rnd, slot, lo, hi):
        for step in range(owners):
            share_out[rnd, step, lo:hi] = slot_image[slot_for((owner + step) % owners), lo:hi]
        for step in range(1, owners):
            share_copy(rnd, slot, lo, hi, step, 1, any_mate(step)).start()

    def finish_image(rnd, slot, lo, hi):
        share_copy(rnd, slot, lo, hi, 1, owners - 1, ahead).wait_recv()
        total = share_out[rnd, 0, lo:hi]
        for step in range(1, owners):
            total = total + share_in[rnd, step, lo:hi]
        images_ref[rnd, lo:hi] = total

    def drain_share(rnd, slot, lo, hi):
        share_copy(rnd, slot, lo, hi, 1, owners - 1, ahead).wait_send()

    def tail_slot(piece):
        return final % share_slots if piece == 0 else share_slots + piece - 1

    @pl.loop(0, HANDOVERS)
    def _(rnd):
        for freq in range(freqs):
            closing = freq == freqs - 1
            have = 0
            sent = 0
            shared = 0
            for group, (lo, hi) in enumerate(groups):
                need = min(hi + reach, nblk)
                fresh = []
                while have < len(parts) and (parts[have][0] < need):
                    fresh.append(have)
                    have += 1

                opening = freq == 0 and group == 0

                @pl.when(rnd == 0)
                def _():
                    if group == 0:
                        unpack_front(freq)
                    if not opening:
                        take(freq, lo, hi)

                @pl.when(rnd > 0)
                def _():
                    for part in fresh:
                        start, end = parts[part]
                        wave_copy(rnd - 1, freq, part).wait_recv()
                        padded[freq, reach + start : reach + end] = inbox[
                            rnd - 1, freq, start:end
                        ]

                for start, end in first if opening else [(lo, hi)]:
                    if opening:

                        @pl.when(rnd == 0)
                        def _():
                            take(freq, start, end)

                    for b in range(start, end):
                        one_block(rnd, freq, b)

                    if opening:

                        @pl.when(rnd == 0)
                        def _():
                            if start == 0:
                                pl.semaphore_wait(barrier, len(greeted))
                                assign_load.wait()
                            wave_copy(rnd, freq, 0, (start, end)).start()

                outgoing = []
                while sent < len(parts) and parts[sent][1] <= hi:
                    outgoing.append(sent)
                    sent += 1

                if outgoing:

                    @pl.when((rnd >= send_slots) & (rnd < final))
                    def _():
                        for part in outgoing:
                            wave_copy(rnd - send_slots, freq, part).wait_send()

                    @pl.when((rnd >= int(opening)) & (rnd < final))
                    def _():
                        for part in outgoing:
                            wave_copy(rnd, freq, part).start()

                @pl.when(rnd == final)
                def _():
                    nonlocal shared
                    while closing and shared < len(tails) and tails[shared][1] <= hi:
                        send_share(rnd, tail_slot(shared), *tails[shared])
                        shared += 1
                    for b in range(lo, hi):
                        cols = slice(b * block, (b + 1) * block)
                        for c in range(nfield):
                            rows = slice(c * slots, (c + 1) * slots)
                            last_ref[c, freq, :, cols] = outbox[rnd, freq, b, rows, :]

            if freq == WHERE:

                @pl.when(rnd >= LAG)
                def _():
                    before = rnd - LAG
                    finish_image(before, before % share_slots, 0, nblk)
                    drain_share(before, before % share_slots, 0, nblk)

        @pl.when(rnd < final)
        def _():
            send_share(rnd, rnd % share_slots, 0, nblk)

    for rnd in range(max(final - send_slots, 0), final):
        for freq in range(freqs):
            for part in range(len(parts)):
                wave_copy(rnd, freq, part).wait_send()
    for rnd in range(max(HANDOVERS - LAG, 0), final):
        finish_image(rnd, rnd % share_slots, 0, nblk)
        drain_share(rnd, rnd % share_slots, 0, nblk)
    for piece, (lo, hi) in enumerate(tails):
        finish_image(final, tail_slot(piece), lo, hi)
    for piece, (lo, hi) in enumerate(tails):
        drain_share(final, tail_slot(piece), lo, hi)


def store(images_ref, last_ref, images_hbm, last_hbm, sem):
    copies = [
        pltpu.make_async_copy(last_ref, last_hbm, sem.at[0]),
        pltpu.make_async_copy(images_ref, images_hbm, sem.at[1]),
    ]
    for copy in copies:
        copy.start()
    for copy in copies:
        copy.wait()


def on_device(sections, owners, fronts, extrap, offsets, assign):
    nfield, freqs, slots, points = fronts.shape
    _, nblk, band, _, block, _ = extrap.shape
    moves = HANDOVERS - 1
    wave = (moves, freqs, nblk, nfield * slots, block)
    share = (HANDOVERS, owners, nblk, block)
    wave_slots = min(2 if sections == 2 else moves, moves)
    send_slots = SENDS or wave_slots
    parts, tails = (len(cuts(nblk, e)) for e in (PART_ENDS, TAIL_ENDS))
    vmem = pl.BlockSpec(memory_space=pltpu.VMEM)
    hbm = pl.BlockSpec(memory_space=pltpu.HBM)
    dma = pltpu.SemaphoreType.DMA
    shapes = (
        jax.ShapeDtypeStruct((HANDOVERS, nblk, block), jnp.float32),
        jax.ShapeDtypeStruct(fronts.shape, fronts.dtype),
    )
    held = [
        pltpu.with_memory_space_constraint(a, pltpu.HBM) for a in (offsets, assign, fronts, extrap)
    ]
    images, last = pl.pallas_call(
        functools.partial(kernel, sections, owners),
        out_shape=shapes,
        in_specs=[hbm] * 4,
        out_specs=(vmem, vmem),
        scratch_shapes=[
            pltpu.SMEM(offsets.shape, offsets.dtype),
            pltpu.SMEM(assign.shape, assign.dtype),
            pltpu.VMEM(fronts.shape, fronts.dtype),
            pltpu.VMEM(extrap.shape, extrap.dtype),
            pltpu.VMEM((freqs, nblk + 2 * (band // 2), nfield * slots, block), fronts.dtype),
            pltpu.VMEM((HANDOVERS,) + wave[1:], fronts.dtype),
            pltpu.VMEM(wave, fronts.dtype),
            pltpu.VMEM((nblk, slots, block), jnp.float32),
            pltpu.VMEM((slots, nblk, block), jnp.float32),
            pltpu.VMEM(share, jnp.float32),
            pltpu.VMEM(share, jnp.float32),
            dma((2,)),
            dma((freqs,)),
            dma((DEEP,)),
            dma((send_slots, freqs, parts)),
            dma((wave_slots, freqs, parts)),
            dma((2 * LAG + tails - 1,)),
            dma((2 * LAG + tails - 1,)),
        ],
        compiler_params=pltpu.CompilerParams(
            collective_id=0, has_side_effects=True, vmem_limit_bytes=VMEM_BYTES
        ),
    )(*held)
    images, last = pl.pallas_call(
        store,
        out_shape=shapes,
        in_specs=[vmem, vmem],
        out_specs=(hbm, hbm),
        scratch_shapes=[dma((2,))],
        compiler_params=pltpu.CompilerParams(vmem_limit_bytes=STORE_BYTES),
    )(images, last)
    return images.reshape(HANDOVERS, slots // owners, points), last


def solution(mesh):
    depth = mesh.shape["depth"]

    def program(fronts, extrap, offsets, assign):
        sections = offsets.shape[0]
        placed = (
            P(None, ("groups", "depth"), None, None),
            P("depth", None, None, None, None, None),
            P(),
            P(),
        )
        return jax.shard_map(
            functools.partial(on_device, sections, depth // sections),
            mesh=mesh,
            in_specs=placed,
            out_specs=(
                P(None, ("groups", "depth"), None),
                P(None, ("groups", "depth"), None, None),
            ),
            check_vma=False,
        )(fronts, extrap, offsets, assign)

    return program
```
